32 devices in a mesh: rep: 16 (over z, y, core), tp: 2 (over x).
Axes of the slice: x: 2, y: 2, z: 4, core: 2. Of those that a mesh axis runs over, the one named last changes fastest.
Arguments:
- queries: bfloat16 [4096, 8192], P('rep', 'tp'), may hold values from -8 to 8
- cand_keys: bfloat16 [4096, 1024], P('rep', 'tp'), may hold values from -6 to 6
- cand_values: bfloat16 [4096, 1024], P('rep', 'tp'), may hold values from -6 to 6
- prefix_kv: bfloat16 [16, 2, 4096, 1024], P('rep', None, None, 'tp'), may hold values from -8 to 8
- owner: int32 [1], replicated, may hold values from 0 to 15
- lengths: int32 [16, 2], P('rep'), may hold values from 1 to 128, as said below
- out_weight: bfloat16 [8192, 4096], P('tp'), may hold values from -2.390625 to 2.390625
Outputs:
- attn_out: bfloat16 [4096, 4096], P(('rep', 'tp'))
The draws below stay inside these ranges and needn't reach their ends.
Inputs may be any that keep to these rules, and one draw needn't show every extreme that they name: Only the slice of prefix_kv at index owner[0] is read. Candidate c of group g has its real tokens in its first lengths[g, c] slots; the rest are padding.
All inputs are finite; a program needn't handle non-finite values.
Results may differ from the reference program's by a relative error of at most 0.017.
Values may be sent and summed in bfloat16 or wider, within the bound.
A program may use at most 192 MiB of HBM per device.

```python
import math
import jax
import jax.numpy as jnp
from jax import lax

QH = 64
KVH = 8
HD = 128
DWIN = 4096
PREFIX = 4096
CLEN = 128
CANDS = 2
GROUPS = 16
ROWS = 256
TOTAL_ROWS = 4096
N_TP = 2


def draw_queries(key, part):
    array_shape = (TOTAL_ROWS, QH * HD)
    values = jnp.clip(jax.random.normal(jax.random.fold_in(key, 1), array_shape, jnp.float32), -6.0, 6.0)
    return values.astype(jnp.bfloat16)


def draw_prefix_kv(key, part):
    array_shape = (GROUPS, 2, PREFIX, KVH * HD)
    values = jnp.clip(jax.random.normal(jax.random.fold_in(key, 2), array_shape, jnp.float32), -6.0, 6.0)
    return values.astype(jnp.bfloat16)


def draw_lengths(key, part):
    counts = jax.random.randint(jax.random.fold_in(key, 3), (GROUPS * CANDS,), 1, CLEN + 1, dtype=jnp.int32)
    chosen = jax.random.randint(jax.random.fold_in(key, 4), (), 0, GROUPS * CANDS, dtype=jnp.int32)
    counts = counts.at[chosen].set(CLEN)
    return counts.reshape(GROUPS, CANDS)


def levels(key, shape, split, least, top_value):
    gain, own = 1.0, jax.random.fold_in(key, 6)
    for dim, shards_of in split:
        steps = jnp.exp(jax.random.uniform(jax.random.fold_in(own, dim), (shards_of,), jnp.float32, least / len(split), top_value / len(split)))
        gain = gain * jnp.repeat(steps, shape[dim] // shards_of).reshape([-1 if axis == dim else 1 for axis in range(len(shape))])
    return gain


def normal_values(own_key, shape, spread, limit, cuts=(), kind=jnp.bfloat16):
    values = spread * jax.random.normal(own_key, shape, jnp.float32)
    if cuts:
        values = values * levels(own_key, shape, cuts, -0.22, 0.18)
    return jnp.clip(values, -limit, limit).astype(kind)


def setup_inputs(seed: int = 0) -> dict:
    key_of = jax.random.split(jax.random.key(seed), 8)
    return {
        "queries": draw_queries(jax.random.fold_in(key_of[7], 71), 0),
        "cand_keys": normal_values(key_of[1], (TOTAL_ROWS, KVH * HD), 1.0, 6.0, ((0, 16), (1, 2))),
        "cand_values": normal_values(key_of[2], (TOTAL_ROWS, KVH * HD), 1.0, 6.0, ((0, 16), (1, 2))),
        "prefix_kv": draw_prefix_kv(jax.random.fold_in(key_of[7], 71), 0),
        "owner": jax.random.randint(key_of[4], (1,), 0, GROUPS).astype(jnp.int32),
        "lengths": draw_lengths(jax.random.fold_in(key_of[7], 71), 0),
        "out_weight": normal_values(key_of[6], (QH * HD, DWIN), 0.4, 2.390625, ((0, 2),)),
    }


NEG = -1e+30

def group_context(inputs, prefix_keys, prefix_values):
    group_queries, own_keys, own_values, cand_lengths = inputs
    head_group = QH // KVH
    score_scale = 1.0 / math.sqrt(HD)
    query_grid = group_queries.astype(jnp.float32).reshape(ROWS, KVH, head_group, HD)
    key_prefix = prefix_keys.astype(jnp.float32).reshape(PREFIX, KVH, HD)
    value_prefix = prefix_values.astype(jnp.float32).reshape(PREFIX, KVH, HD)
    prefix_scores = jnp.einsum('rkgd,pkd->kgrp', query_grid, key_prefix) * score_scale
    cand_queries = query_grid.reshape(CANDS, CLEN, KVH, head_group, HD)
    key_grid = own_keys.astype(jnp.float32).reshape(CANDS, CLEN, KVH, HD)
    value_grid = own_values.astype(jnp.float32).reshape(CANDS, CLEN, KVH, HD)
    own_scores = jnp.einsum('cikgd,cjkd->kgcij', cand_queries, key_grid) * score_scale
    live_mask = jnp.arange(CLEN, dtype=jnp.int32)[None, :] < cand_lengths[:, None]
    own_scores = jnp.where(live_mask[None, None, :, None, :], own_scores, NEG)
    row_max = jnp.maximum(lax.optimization_barrier(jnp.max(prefix_scores, -1)), lax.optimization_barrier(jnp.max(own_scores, -1)).reshape(KVH, head_group, ROWS))
    expo_prefix = jnp.exp(prefix_scores - row_max[..., None])
    expo_own = jnp.exp(own_scores - row_max.reshape(KVH, head_group, CANDS, CLEN)[..., None])
    row_total = lax.optimization_barrier(jnp.sum(expo_prefix, -1)) + lax.optimization_barrier(jnp.sum(expo_own, -1)).reshape(KVH, head_group, ROWS)
    weight_prefix = lax.optimization_barrier(expo_prefix.astype(jnp.bfloat16)).astype(jnp.float32)
    weight_own = lax.optimization_barrier(expo_own.astype(jnp.bfloat16)).astype(jnp.float32)
    weighted = jnp.einsum('kgrp,pkd->kgrd', weight_prefix, value_prefix)
    weighted = weighted + jnp.einsum('kgcij,cjkd->kgcid', weight_own, value_grid).reshape(KVH, head_group, ROWS, HD)
    context = weighted / row_total[..., None]
    context = jnp.transpose(context, (2, 0, 1, 3)).reshape(ROWS, QH * HD)
    return lax.optimization_barrier(context.astype(jnp.bfloat16))

def reference(queries, cand_keys, cand_values, prefix_kv, owner, lengths, out_weight):
    prefix = lax.dynamic_index_in_dim(prefix_kv, owner[0].astype(jnp.int32), 0, keepdims=False)
    weight_parts = out_weight.astype(jnp.float32).reshape(N_TP, QH * HD // N_TP, DWIN)

    def per_group(inputs):
        context = group_context(inputs, prefix[0], prefix[1])
        context_parts = context.astype(jnp.float32).reshape(ROWS, N_TP, QH * HD // N_TP)
        partial_value = jnp.einsum('rtc,tcd->trd', context_parts, weight_parts)
        rounded = lax.optimization_barrier(partial_value.astype(jnp.bfloat16)).astype(jnp.float32)
        return lax.optimization_barrier(jnp.sum(rounded, 0)).astype(jnp.bfloat16)
    grouped = lax.map(per_group, (queries.reshape(GROUPS, ROWS, QH * HD), cand_keys.reshape(GROUPS, ROWS, KVH * HD), cand_values.reshape(GROUPS, ROWS, KVH * HD), lengths))
    return grouped.reshape(GROUPS * ROWS, DWIN)
```

```python
import functools
import math

import jax
import jax.numpy as jnp
from jax import lax
from jax.experimental import pallas as pl
from jax.experimental.pallas import tpu as pltpu
from jax.sharding import PartitionSpec as P

QH = 64
KVH = 8
HD = 128
CLEN = 128
NEG = -1e30
MESH = pl.DeviceIdType.MESH


def plan(root, ranks):
    chips = ranks // 2
    lines = chips // 2
    rz, ry = (root // 2) // 2, (root // 2) % 2
    oy = 1 - ry
    rank = lambda z, y, c: (z * 2 + y) * 2 + c
    passes = [[] for _ in range(ranks)]
    sib = root ^ 1

    def edge(s, src, dst):
        source = root if src == (rz, ry) else rank(*src, s)
        passes[source].append((s, rank(*dst, s)))

    for s, row in ((0, ry), (1, oy)):
        for z in range(rz, lines - 1):
            edge(s, (z, row), (z + 1, row))
        for z in range(rz, 0, -1):
            edge(s, (z, row), (z - 1, row))
        for z in range(lines):
            if z != rz:
                edge(s, (z, row), (z, 1 - row))
    back = rz + 1 if rz + 1 < lines else rz - 1
    edge(0, (back, oy), (rz, oy))
    edge(1, (rz, ry), (rz, oy))
    for i in range(ranks):
        if i == root:
            passes[i] += [(0, sib), (1, sib)]
        elif i == sib:
            passes[i] += [(0, root), (1, root)]
        else:
            passes[i].append((i % 2, i ^ 1))
    return passes


def bcast_kernel(root, ranks, chunks, x_ref, o_ref, send_sem, recv_sem):
    me = lax.axis_index("rep")
    passes = plan(root, ranks)
    half = x_ref.shape[1] // 2
    width = half // chunks
    near = [set(t for _, t in passes[i]) for i in range(ranks)]
    for i in range(ranks):
        for t in list(near[i]):
            near[t].add(i)

    def piece(ref, s, k):
        return ref.at[:, pl.ds(pl.multiple_of(s * half + k * width, width), width), :]

    def copy(ref, s, k, slot, target):
        return pltpu.make_async_remote_copy(
            src_ref=piece(ref, s, k),
            dst_ref=piece(o_ref, s, k),
            send_sem=send_sem.at[slot],
            recv_sem=recv_sem.at[s, k],
            device_id={"rep": target},
            device_id_type=MESH,
        )

    barrier = pltpu.get_barrier_semaphore()

    for i in range(ranks):

        @pl.when(me == i)
        def _(i=i):
            for t in sorted(near[i]):
                pl.semaphore_signal(barrier, inc=1, device_id={"rep": t}, device_id_type=MESH)
            pl.semaphore_wait(barrier, len(near[i]))
            ref = x_ref if i == root else o_ref
            streams = sorted(set(s for s, _ in passes[i]))

            def step(k, carry):
                for s in streams:
                    if i != root:
                        copy(ref, s, k, 0, root).wait_recv()
                    for slot, (t_s, t) in enumerate(passes[i]):
                        if t_s == s:
                            copy(ref, s, k, slot, t).start()
                return carry

            lax.fori_loop(0, chunks, step, 0)

            def rest(k, carry):
                for s in (0, 1):
                    if i == root or s not in streams:
                        copy(ref, s, k, 0, root ^ 1).wait_recv()
                return carry

            lax.fori_loop(0, chunks, rest, 0)
            for slot, (s, t) in enumerate(passes[i]):
                whole = ref.at[:, pl.ds(s * half, half), :]
                pltpu.make_async_remote_copy(
                    src_ref=whole,
                    dst_ref=whole,
                    send_sem=send_sem.at[slot],
                    recv_sem=recv_sem.at[s, 0],
                    device_id={"rep": t},
                    device_id_type=MESH,
                ).wait_send()


def broadcast(shard, owner_index, ranks):
    half = shard.shape[1] // 2
    chunks = max(1, min(32, half // 16))

    def branch(root):
        def call(x):
            return pl.pallas_call(
                functools.partial(bcast_kernel, root, ranks, chunks),
                out_shape=jax.ShapeDtypeStruct(x.shape, x.dtype),
                in_specs=[pl.BlockSpec(memory_space=pl.ANY)],
                out_specs=pl.BlockSpec(memory_space=pl.ANY),
                scratch_shapes=[
                    pltpu.SemaphoreType.DMA((8,)),
                    pltpu.SemaphoreType.DMA((2, chunks)),
                ],
                compiler_params=pltpu.CompilerParams(
                    collective_id=1 + root, has_side_effects=True
                ),
            )(x)

        return call

    return lax.switch(owner_index, [branch(r) for r in range(ranks)], shard)


def attend_kernel(head_group, len_ref, q_ref, ck_ref, cv_ref, pk_ref, pv_ref, o_ref, vone, cone):
    rows = q_ref.shape[0]
    prefix_len = pk_ref.shape[1]
    block = min(1024, prefix_len)
    rate = math.log2(math.e) / math.sqrt(HD)
    vone[:, :HD] = pv_ref[0]
    vone[:, HD:] = jnp.ones((prefix_len, HD), vone.dtype)
    cone[:, :HD] = cv_ref[...]
    cone[:, HD:] = jnp.ones((rows, HD), cone.dtype)
    row_cand = lax.broadcasted_iota(jnp.int32, (rows, rows), 0) // CLEN
    col = lax.broadcasted_iota(jnp.int32, (rows, rows), 1)
    length = jnp.zeros((rows, rows), jnp.int32)
    for c in range(rows // CLEN):
        length = jnp.where(row_cand == c, c * CLEN + len_ref[0, c], length)
    live = (col >= row_cand * CLEN) & (col < length)

    def qk(q, k):
        return lax.dot_general(q, k, (((1,), (1,)), ((), ())), preferred_element_type=jnp.float32)

    def head(g, carry):
        cols = pl.ds(pl.multiple_of(g * HD, HD), HD)
        q = q_ref[:, cols]
        pieces = prefix_len // block
        score = jnp.where(live, qk(q, ck_ref[...]), NEG)
        top = None
        for b in range(pieces + 1):
            if b < pieces:
                ahead = qk(q, pk_ref[0, b * block : (b + 1) * block, :])
            value = cone[...] if b == 0 else vone[(b - 1) * block : b * block, :]
            peak = jnp.max(score, -1, keepdims=True)
            if b == 0:
                top = peak
            else:
                fresh = jnp.maximum(top, peak)
                factor = jnp.exp2((top - fresh) * rate)
                top = fresh
            weight = jnp.exp2((score - top) * rate).astype(jnp.bfloat16)
            part = jnp.dot(weight, value, preferred_element_type=jnp.float32)
            acc = part if b == 0 else acc * factor + part
            score = ahead
        o_ref[:, cols] = (acc[:, :HD] / acc[:, HD:]).astype(o_ref.dtype)
        return carry

    lax.fori_loop(0, head_group, head, 0)


def attend(queries, cand_keys, cand_values, prefix, lengths):
    rows = queries.shape[0]
    kv_heads = cand_keys.shape[1] // HD
    head_group = QH // KVH
    prefix_len = prefix.shape[1]
    wide = head_group * HD
    return pl.pallas_call(
        functools.partial(attend_kernel, head_group),
        grid=(kv_heads,),
        out_shape=jax.ShapeDtypeStruct(queries.shape, jnp.bfloat16),
        in_specs=[
            pl.BlockSpec(memory_space=pltpu.SMEM),
            pl.BlockSpec((rows, wide), lambda h: (0, h)),
            pl.BlockSpec((rows, HD), lambda h: (0, h)),
            pl.BlockSpec((rows, HD), lambda h: (0, h)),
            pl.BlockSpec((1, prefix_len, HD), lambda h: (0, 0, h)),
            pl.BlockSpec((1, prefix_len, HD), lambda h: (1, 0, h)),
        ],
        out_specs=pl.BlockSpec((rows, wide), lambda h: (0, h)),
        scratch_shapes=[
            pltpu.VMEM((prefix_len, 2 * HD), jnp.bfloat16),
            pltpu.VMEM((rows, 2 * HD), jnp.bfloat16),
        ],
    )(lengths, queries, cand_keys, cand_values, prefix, prefix)


def project_kernel(n, tiles, c_ref, w_ref, o_ref, stage, landed, send_sem, recv_sem):
    j = pl.program_id(0)
    me = lax.axis_index("tp")
    rows, width = landed.shape[2], landed.shape[3]

    @pl.when(j == 0)
    def _():
        barrier = pltpu.get_barrier_semaphore()
        for o in range(1, n):
            pl.semaphore_signal(
                barrier, inc=1, device_id={"tp": lax.rem(me + o, n)}, device_id_type=MESH
            )
        pl.semaphore_wait(barrier, n - 1)

    stage[j] = jnp.dot(c_ref[...], w_ref[...], preferred_element_type=jnp.float32).astype(
        stage.dtype
    )

    def copy(t, o):
        peer = lax.rem(me + o, n)
        return pltpu.make_async_remote_copy(
            src_ref=stage.at[t, pl.ds(pl.multiple_of(peer * rows, rows), rows), :],
            dst_ref=landed.at[t, o - 1],
            send_sem=send_sem.at[t, o - 1],
            recv_sem=recv_sem.at[t, o - 1],
            device_id={"tp": peer},
            device_id_type=MESH,
        )

    for o in range(1, n):
        copy(j, o).start()

    def finish(t):
        total = stage[t, pl.ds(pl.multiple_of(me * rows, rows), rows), :].astype(jnp.float32)
        for o in range(1, n):
            copy(t, o).wait_recv()
            total += landed[t, o - 1].astype(jnp.float32)
        o_ref[:, pl.ds(pl.multiple_of(t * width, width), width)] = total.astype(o_ref.dtype)

    @pl.when(j > 0)
    def _():
        finish(j - 1)

    @pl.when(j == tiles - 1)
    def _():
        finish(j)

        def drain(t, carry):
            for o in range(1, n):
                copy(t, o).wait_send()
            return carry

        lax.fori_loop(0, tiles, drain, 0)


def project(context, out_weight, n):
    row_count = context.shape[0]
    rows = row_count // n
    depth, columns = out_weight.shape
    width = min(512, columns)
    tiles = columns // width
    return pl.pallas_call(
        functools.partial(project_kernel, n, tiles),
        grid=(tiles,),
        out_shape=jax.ShapeDtypeStruct((rows, columns), jnp.bfloat16),
        in_specs=[
            pl.BlockSpec((row_count, depth), lambda j: (0, 0)),
            pl.BlockSpec((depth, width), lambda j: (0, j)),
        ],
        out_specs=pl.BlockSpec((rows, columns), lambda j: (0, 0)),
        scratch_shapes=[
            pltpu.VMEM((tiles, row_count, width), jnp.bfloat16),
            pltpu.VMEM((tiles, n - 1, rows, width), jnp.bfloat16),
            pltpu.SemaphoreType.DMA((tiles, n - 1)),
            pltpu.SemaphoreType.DMA((tiles, n - 1)),
        ],
        compiler_params=pltpu.CompilerParams(collective_id=0, has_side_effects=True),
    )(context, out_weight)


def solution(mesh):
    ranks, n = mesh.shape["rep"], mesh.shape["tp"]

    def body(queries, cand_keys, cand_values, prefix_kv, owner, lengths, out_weight):
        arrived = broadcast(prefix_kv[0], owner[0], ranks)
        context = attend(queries, cand_keys, cand_values, arrived, lengths)
        return project(context, out_weight, n)

    in_specs = (
        P("rep", "tp"),
        P("rep", "tp"),
        P("rep", "tp"),
        P("rep", None, None, "tp"),
        P(),
        P("rep", None),
        P("tp", None),
    )
    out_specs = P(("rep", "tp"), None)
    return jax.shard_map(body, mesh=mesh, in_specs=in_specs, out_specs=out_specs, check_vma=False)
```

```python
import functools
import math

import jax
import jax.numpy as jnp
from jax import lax
from jax.experimental import pallas as pl
from jax.experimental.pallas import tpu as pltpu
from jax.sharding import PartitionSpec as P

QH = 64
KVH = 8
HD = 128
CLEN = 128
NEG = -1e30
MESH = pl.DeviceIdType.MESH


def plan(root, ranks):
    chips = ranks // 2
    lines = chips // 2
    rz, ry = (root // 2) // 2, (root // 2) % 2
    oy = 1 - ry
    rank = lambda z, y, c: (z * 2 + y) * 2 + c
    passes = [[] for _ in range(ranks)]
    sib = root ^ 1

    def edge(s, src, dst):
        source = root if src == (rz, ry) else rank(*src, s)
        passes[source].append((s, rank(*dst, s)))

    for s, row in ((0, ry), (1, oy)):
        for z in range(rz, lines - 1):
            edge(s, (z, row), (z + 1, row))
        for z in range(rz, 0, -1):
            edge(s, (z, row), (z - 1, row))
        for z in range(lines):
            if z != rz:
                edge(s, (z, row), (z, 1 - row))
    back = rz + 1 if rz + 1 < lines else rz - 1
    edge(0, (back, oy), (rz, oy))
    edge(1, (rz, ry), (rz, oy))
    for i in range(ranks):
        if i == root:
            passes[i] += [(0, sib), (1, sib)]
        elif i == sib:
            passes[i] += [(0, root), (1, root)]
        else:
            passes[i].append((i % 2, i ^ 1))
    return passes


def bcast_kernel(root, ranks, chunks, x_ref, o_ref, send_sem, recv_sem):
    me = lax.axis_index("rep")
    passes = plan(root, ranks)
    half = x_ref.shape[1] // 2
    width = half // chunks
    near = [set(t for _, t in passes[i]) for i in range(ranks)]
    for i in range(ranks):
        for t in list(near[i]):
            near[t].add(i)

    def piece(ref, s, k):
        return ref.at[:, pl.ds(pl.multiple_of(s * half + k * width, width), width), :]

    def copy(ref, s, k, slot, target):
        return pltpu.make_async_remote_copy(
            src_ref=piece(ref, s, k),
            dst_ref=piece(o_ref, s, k),
            send_sem=send_sem.at[slot],
            recv_sem=recv_sem.at[s, k],
            device_id={"rep": target},
            device_id_type=MESH,
        )

    barrier = pltpu.get_barrier_semaphore()

    for i in range(ranks):

        @pl.when(me == i)
        def _(i=i):
            for t in sorted(near[i]):
                pl.semaphore_signal(barrier, inc=1, device_id={"rep": t}, device_id_type=MESH)
            pl.semaphore_wait(barrier, len(near[i]))
            ref = x_ref if i == root else o_ref
            streams = sorted(set(s for s, _ in passes[i]))

            def step(k, carry):
                for s in streams:
                    if i != root:
                        copy(ref, s, k, 0, root).wait_recv()
                    for slot, (t_s, t) in enumerate(passes[i]):
                        if t_s == s:
                            copy(ref, s, k, slot, t).start()
                return carry

            lax.fori_loop(0, chunks, step, 0)

            def rest(k, carry):
                for s in (0, 1):
                    if i == root or s not in streams:
                        copy(ref, s, k, 0, root ^ 1).wait_recv()
                return carry

            lax.fori_loop(0, chunks, rest, 0)
            for slot, (s, t) in enumerate(passes[i]):
                whole = ref.at[:, pl.ds(s * half, half), :]
                pltpu.make_async_remote_copy(
                    src_ref=whole,
                    dst_ref=whole,
                    send_sem=send_sem.at[slot],
                    recv_sem=recv_sem.at[s, 0],
                    device_id={"rep": t},
                    device_id_type=MESH,
                ).wait_send()


def broadcast(shard, owner_index, ranks):
    half = shard.shape[1] // 2
    chunks = max(1, min(32, half // 16))

    def branch(root):
        def call(x):
            return pl.pallas_call(
                functools.partial(bcast_kernel, root, ranks, chunks),
                out_shape=jax.ShapeDtypeStruct(x.shape, x.dtype),
                in_specs=[pl.BlockSpec(memory_space=pl.ANY)],
                out_specs=pl.BlockSpec(memory_space=pl.ANY),
                scratch_shapes=[
                    pltpu.SemaphoreType.DMA((8,)),
                    pltpu.SemaphoreType.DMA((2, chunks)),
                ],
                compiler_params=pltpu.CompilerParams(
                    collective_id=1 + root, has_side_effects=True
                ),
            )(x)

        return call

    return lax.switch(owner_index, [branch(r) for r in range(ranks)], shard)


def attend_kernel(head_group, len_ref, q_ref, ck_ref, cv_ref, pk_ref, pv_ref, o_ref, vone, cone):
    rows = q_ref.shape[0]
    prefix_len = pk_ref.shape[1]
    block = min(1024, prefix_len)
    rate = math.log2(math.e) / math.sqrt(HD)
    vone[:, :HD] = pv_ref[0]
    vone[:, HD:] = jnp.ones((prefix_len, HD), vone.dtype)
    cone[:, :HD] = cv_ref[...]
    cone[:, HD:] = jnp.ones((rows, HD), cone.dtype)
    row_cand = lax.broadcasted_iota(jnp.int32, (rows, rows), 0) // CLEN
    col = lax.broadcasted_iota(jnp.int32, (rows, rows), 1)
    length = jnp.zeros((rows, rows), jnp.int32)
    for c in range(rows // CLEN):
        length = jnp.where(row_cand == c, c * CLEN + len_ref[0, c], length)
    live = (col >= row_cand * CLEN) & (col < length)

    def qk(q, k):
        return lax.dot_general(q, k, (((1,), (1,)), ((), ())), preferred_element_type=jnp.float32)

    def head(g, carry):
        cols = pl.ds(pl.multiple_of(g * HD, HD), HD)
        q = q_ref[:, cols]
        pieces = prefix_len // block
        score = jnp.where(live, qk(q, ck_ref[...]), NEG)
        top = None
        for b in range(pieces + 1):
            if b < pieces:
                ahead = qk(q, pk_ref[0, b * block : (b + 1) * block, :])
            value = cone[...] if b == 0 else vone[(b - 1) * block : b * block, :]
            peak = jnp.max(score, -1, keepdims=True)
            if b == 0:
                top = peak
            else:
                fresh = jnp.maximum(top, peak)
                factor = jnp.exp2((top - fresh) * rate)
                top = fresh
            weight = jnp.exp2((score - top) * rate).astype(jnp.bfloat16)
            part = jnp.dot(weight, value, preferred_element_type=jnp.float32)
            acc = part if b == 0 else acc * factor + part
            score = ahead
        o_ref[:, cols] = (acc[:, :HD] / acc[:, HD:]).astype(o_ref.dtype)
        return carry

    lax.fori_loop(0, head_group, head, 0, unroll=2)


def attend(queries, cand_keys, cand_values, prefix, lengths):
    rows = queries.shape[0]
    kv_heads = cand_keys.shape[1] // HD
    head_group = QH // KVH
    prefix_len = prefix.shape[1]
    wide = head_group * HD
    return pl.pallas_call(
        functools.partial(attend_kernel, head_group),
        grid=(kv_heads,),
        out_shape=jax.ShapeDtypeStruct(queries.shape, jnp.bfloat16),
        in_specs=[
            pl.BlockSpec(memory_space=pltpu.SMEM),
            pl.BlockSpec((rows, wide), lambda h: (0, h)),
            pl.BlockSpec((rows, HD), lambda h: (0, h)),
            pl.BlockSpec((rows, HD), lambda h: (0, h)),
            pl.BlockSpec((1, prefix_len, HD), lambda h: (0, 0, h)),
            pl.BlockSpec((1, prefix_len, HD), lambda h: (1, 0, h)),
        ],
        out_specs=pl.BlockSpec((rows, wide), lambda h: (0, h)),
        scratch_shapes=[
            pltpu.VMEM((prefix_len, 2 * HD), jnp.bfloat16),
            pltpu.VMEM((rows, 2 * HD), jnp.bfloat16),
        ],
    )(lengths, queries, cand_keys, cand_values, prefix, prefix)


def project_kernel(n, tiles, c_ref, w_ref, o_ref, stage, landed, send_sem, recv_sem):
    j = pl.program_id(0)
    me = lax.axis_index("tp")
    rows, width = landed.shape[2], landed.shape[3]

    @pl.when(j == 0)
    def _():
        barrier = pltpu.get_barrier_semaphore()
        for o in range(1, n):
            pl.semaphore_signal(
                barrier, inc=1, device_id={"tp": lax.rem(me + o, n)}, device_id_type=MESH
            )
        pl.semaphore_wait(barrier, n - 1)

    stage[j] = jnp.dot(c_ref[...], w_ref[...], preferred_element_type=jnp.float32).astype(
        stage.dtype
    )

    def copy(t, o):
        peer = lax.rem(me + o, n)
        return pltpu.make_async_remote_copy(
            src_ref=stage.at[t, pl.ds(pl.multiple_of(peer * rows, rows), rows), :],
            dst_ref=landed.at[t, o - 1],
            send_sem=send_sem.at[t, o - 1],
            recv_sem=recv_sem.at[t, o - 1],
            device_id={"tp": peer},
            device_id_type=MESH,
        )

    for o in range(1, n):
        copy(j, o).start()

    def finish(t):
        total = stage[t, pl.ds(pl.multiple_of(me * rows, rows), rows), :].astype(jnp.float32)
        for o in range(1, n):
            copy(t, o).wait_recv()
            total += landed[t, o - 1].astype(jnp.float32)
        o_ref[:, pl.ds(pl.multiple_of(t * width, width), width)] = total.astype(o_ref.dtype)

    lag = min(3, tiles - 1)

    @pl.when(j >= lag)
    def _():
        finish(j - lag)

    @pl.when(j == tiles - 1)
    def _():
        for t in range(tiles - lag, tiles):
            finish(t)

        def drain(t, carry):
            for o in range(1, n):
                copy(t, o).wait_send()
            return carry

        lax.fori_loop(0, tiles, drain, 0)


def project(context, out_weight, n):
    row_count = context.shape[0]
    rows = row_count // n
    depth, columns = out_weight.shape
    width = min(512, columns)
    tiles = columns // width
    return pl.pallas_call(
        functools.partial(project_kernel, n, tiles),
        grid=(tiles,),
        out_shape=jax.ShapeDtypeStruct((rows, columns), jnp.bfloat16),
        in_specs=[
            pl.BlockSpec((row_count, depth), lambda j: (0, 0)),
            pl.BlockSpec((depth, width), lambda j: (0, j)),
        ],
        out_specs=pl.BlockSpec((rows, columns), lambda j: (0, 0)),
        scratch_shapes=[
            pltpu.VMEM((tiles, row_count, width), jnp.bfloat16),
            pltpu.VMEM((tiles, n - 1, rows, width), jnp.bfloat16),
            pltpu.SemaphoreType.DMA((tiles, n - 1)),
            pltpu.SemaphoreType.DMA((tiles, n - 1)),
        ],
        compiler_params=pltpu.CompilerParams(collective_id=0, has_side_effects=True),
    )(context, out_weight)


def solution(mesh):
    ranks, n = mesh.shape["rep"], mesh.shape["tp"]

    def body(queries, cand_keys, cand_values, prefix_kv, owner, lengths, out_weight):
        arrived = broadcast(prefix_kv[0], owner[0], ranks)
        context = attend(queries, cand_keys, cand_values, arrived, lengths)
        return project(context, out_weight, n)

    in_specs = (
        P("rep", "tp"),
        P("rep", "tp"),
        P("rep", "tp"),
        P("rep", None, None, "tp"),
        P(),
        P("rep", None),
        P("tp", None),
    )
    out_specs = P(("rep", "tp"), None)
    return jax.shard_map(body, mesh=mesh, in_specs=in_specs, out_specs=out_specs, check_vma=False)
```
